256 devices in a mesh: sub: 32 (over z_hi, y, core), grp: 8 (over z_lo, x).
Axes of the slice: x: 4, y: 4, z: 8 (z_hi: 4, z_lo: 2; z = z_hi * 2 + z_lo), core: 2. Of those that a mesh axis runs over, the one named last changes fastest.
Arguments:
- right_side: float32 [8, 32, 1024, 128], P('grp', 'sub'), may hold values from -13 to 13
- schur_blocks: bfloat16 [8, 32, 2048, 2048], P('grp', 'sub'), may hold values from -2 to 7, as said below
- occupancy: int32 [8, 32, 1024], P('grp', 'sub'), may hold values 0 or 1
- precond_weights: float32 [8, 32, 1024], P('grp', 'sub'), may hold values from 0.1 to 1
- coarse_basis: float32 [8, 32, 8, 1024], P('grp', 'sub'), may hold values from -0.1875 to 0.1875
- coarse_inverse: float32 [8, 256, 256], P('grp', 'sub'), may hold values from -1 to 5, as said below
Outputs:
- solution: float32 [8, 32, 1024, 128], P('grp', 'sub')
- residual: float32 [8, 32, 1024, 128], P('grp', 'sub')
The draws below stay inside these ranges and needn't reach their ends.
Inputs may be any that keep to these rules, and one draw needn't show every extreme that they name: `schur_blocks`: each strip's block is symmetric positive definite, diagonal entries between 1.4 and 6.1. `coarse_inverse`: each group's matrix is symmetric positive definite, diagonal entries between 0.9 and 4.2.
All inputs are finite; a program needn't handle non-finite values. No bound on the sum of `occupancy` on one device may be relied on, other than what follows from the above.
Results may differ from the reference program's by a relative error of at most 0.035.
Values may be sent and summed in bfloat16 or wider, within the bound.
A program may use at most 64 MiB of HBM per device.

```python
import math
import jax
import jax.numpy as jnp
from jax import lax

F = 1024
K = 2048
GOALS = 128
NC = 8
ITERS = 3
GROUP = 32
GROUPS = 8
STRIPS = 256


def draw_right_side(key, part):
    key_main = jax.random.fold_in(jax.random.fold_in(key, 11), 0)
    strip_pos = jnp.arange(STRIPS, dtype=jnp.float32) / float(STRIPS - 1)
    strip_scale = jnp.exp(math.log(3.0) * strip_pos)[:, None, None]
    values = jnp.clip(jax.random.normal(key_main, (STRIPS, F, GOALS), jnp.float32), -4.0, 4.0)
    return (values * strip_scale).reshape(GROUPS, GROUP, F, GOALS)


def draw_schur_blocks(key, part):
    amplitude = 0.5 / math.sqrt(K)

    def draw_strip(strip_index):
        strip_key = jax.random.fold_in(jax.random.fold_in(key, 23), strip_index)
        key_off, key_diag = jax.random.split(strip_key)
        spread_vals = jax.random.uniform(key_off, (K, K), jnp.float32, -amplitude, amplitude)
        diag_vals = jnp.exp(jax.random.uniform(key_diag, (K,), jnp.float32, math.log(1.5), math.log(6.0)))
        on_diagonal = jnp.arange(K)[:, None] == jnp.arange(K)[None, :]
        matrix = spread_vals + spread_vals.T + jnp.where(on_diagonal, diag_vals[:, None], 0.0)
        return matrix.astype(jnp.bfloat16)
    blocks = lax.map(draw_strip, jnp.arange(STRIPS))
    return blocks.reshape(GROUPS, GROUP, K, K)


def draw_coarse_inverse(key, part):
    order = GROUP * NC
    amplitude = 0.5 / math.sqrt(order)
    key_off, key_diag = jax.random.split(jax.random.fold_in(key, 37))
    spread_vals = jax.random.uniform(key_off, (GROUPS, order, order), jnp.float32, -amplitude, amplitude)
    diag_vals = jnp.exp(jax.random.uniform(key_diag, (GROUPS, order), jnp.float32, 0.0, math.log(4.0)))
    on_diagonal = jnp.arange(order)[:, None] == jnp.arange(order)[None, :]
    return spread_vals + jnp.swapaxes(spread_vals, 1, 2) + jnp.where(on_diagonal[None], diag_vals[:, :, None], 0.0)


def plant(entries, rng, low, high):
    longest = entries.shape.index(max(entries.shape))
    spots = []
    for shift in (0, 1):
        where = [jax.random.randint(jax.random.fold_in(rng, axis), (), 0, length) for axis, length in enumerate(entries.shape)]
        where[longest] = (where[longest] + shift) % entries.shape[longest]
        spots.append(tuple(where))
    return entries.at[spots[0]].set(low).at[spots[1]].set(high)


def steps_of(key, dims, pieces, smallest, high):
    level, own = 1.0, jax.random.fold_in(key, 6)
    for dim, parts in pieces:
        draws = jnp.exp(jax.random.uniform(jax.random.fold_in(own, dim), (parts,), jnp.float32, smallest / len(pieces), high / len(pieces)))
        level = level * jnp.repeat(draws, dims[dim] // parts).reshape([-1 if axis == dim else 1 for axis in range(len(dims))])
    return level


def normal_values(own_key, dims, spread, most, cuts=(), kind=jnp.bfloat16):
    factor_of = steps_of(own_key, dims, cuts, -0.22, 0.18) if cuts else 1.0
    drawn = jax.random.normal(own_key, dims, jnp.float32) * spread * factor_of
    return jnp.minimum(jnp.maximum(drawn, -most), most).astype(kind)


def setup_inputs(seed: int = 0) -> dict:
    streams_of = jax.random.split(jax.random.key(seed), 7)
    return {
        "right_side": draw_right_side(jax.random.fold_in(streams_of[6], 71), 0),
        "schur_blocks": draw_schur_blocks(jax.random.fold_in(streams_of[6], 71), 0),
        "occupancy": plant((jax.random.randint(streams_of[2], (GROUPS, GROUP, F), 0, 8) < 7).astype(jnp.int32), jax.random.fold_in(streams_of[2], 1), 0, 1),
        "precond_weights": jnp.clip(jnp.exp(math.log(1.0) - 2.3025851 * jax.random.uniform(streams_of[3], (GROUPS, GROUP, F), jnp.float32) ** steps_of(streams_of[3], (GROUPS, GROUP, F), ((0, 8), (1, 32)), -0.2, 0.2)), 0.1, 1.0),
        "coarse_basis": normal_values(streams_of[4], (GROUPS, GROUP, NC, F), F ** -0.5, 0.1875, ((0, 8), (1, 32)), jnp.float32),
        "coarse_inverse": draw_coarse_inverse(jax.random.fold_in(streams_of[6], 71), 0),
    }


def apply_operator(vector, schur_blocks, free_cells):
    face_cells = vector.shape[1]
    masked = (free_cells * vector).astype(jnp.bfloat16)
    zero_face = jnp.zeros((1,) + masked.shape[1:], jnp.bfloat16)
    following = jnp.concatenate([masked[1:], zero_face], axis=0)
    extended = jnp.concatenate([masked, following], axis=1)

    def strip_product(pair):
        return jnp.dot(pair[0], pair[1], preferred_element_type=jnp.float32)

    product = lax.map(strip_product, (schur_blocks, extended))
    sent = product[:, face_cells:].astype(jnp.bfloat16)
    incoming = jnp.concatenate([zero_face, sent[:-1]], axis=0).astype(jnp.float32)
    return free_cells * (product[:, :face_cells] + incoming) + (1.0 - free_cells) * vector


def precondition(residual, precond_weights, coarse_basis, coarse_inverse):
    coarse = jnp.einsum('cnf,cfg->cng', coarse_basis, residual, precision=lax.Precision.HIGHEST)
    grouped = coarse.reshape(coarse_inverse.shape[0], coarse_inverse.shape[1], coarse.shape[2])
    solved = jnp.einsum('sij,sjg->sig', coarse_inverse, grouped, precision=lax.Precision.HIGHEST)
    solved = solved.reshape(coarse.shape)
    spread_back = jnp.einsum('cnf,cng->cfg', coarse_basis, solved, precision=lax.Precision.HIGHEST)
    return precond_weights[:, :, None] * residual + spread_back


def reference(right_side, schur_blocks, occupancy, precond_weights, coarse_basis, coarse_inverse):
    out_shape = right_side.shape
    right_flat = right_side.reshape((-1,) + right_side.shape[2:])
    blocks_flat = schur_blocks.reshape((-1,) + schur_blocks.shape[2:])
    free_cells = occupancy.reshape((-1, occupancy.shape[2])).astype(jnp.float32)[:, :, None]
    weights_flat = precond_weights.reshape((-1, precond_weights.shape[2]))
    basis_flat = coarse_basis.reshape((-1,) + coarse_basis.shape[2:])
    solution = jnp.zeros_like(right_flat)
    residual = right_flat
    precond = precondition(residual, weights_flat, basis_flat, coarse_inverse)
    direction = precond
    inner_now = jnp.sum(residual * precond, axis=(0, 1))
    for iteration in range(ITERS):
        image = apply_operator(direction, blocks_flat, free_cells)
        step_size = inner_now / jnp.sum(direction * image, axis=(0, 1))
        solution = solution + step_size * direction
        residual = residual - step_size * image
        if iteration + 1 < ITERS:
            precond = precondition(residual, weights_flat, basis_flat, coarse_inverse)
            inner_next = jnp.sum(residual * precond, axis=(0, 1))
            direction = precond + (inner_next / inner_now) * direction
            inner_now = inner_next
    return solution.reshape(out_shape), residual.reshape(out_shape)
```

```python
import functools

import jax
import jax.numpy as jnp
from jax import lax
from jax.experimental import pallas as pl
from jax.experimental.pallas import tpu as pltpu
from jax.sharding import PartitionSpec as P

ITERS = 3
MESH = pl.DeviceIdType.MESH
F32 = jnp.float32
BF16 = jnp.bfloat16
CH = 256


def split(value):
    high = value.astype(BF16)
    return high, (value - high.astype(F32)).astype(BF16)


def folded(value):
    return jnp.sum(value.reshape(value.shape[0] // 8, 8, value.shape[1]), axis=0)


def place(row):
    return pl.ds(pl.multiple_of(row, CH), CH)


def kernel(
    n_sub, n_grp,
    b_hbm, s_hbm, occ_hbm, w_hbm, basis_hbm, inv_hbm,
    x_ref, r_ref,
    blocks, res, zed, srch, prod, weight, free, masked, held, arrive, leave, half_b,
    own_par, next_par, occ_v, inv, basis_t, spread_rhs, prob, qmat, basis_n, direc,
    coarse_src, coarse_all, kap_src, kap_in, dot_src, dot_grp, dot_mid, dot_sub,
    load_sem, send_sem, par_sem, half_sem, inv_sem, bulk_sem, kap_sem, all_sem, far_sem, grp_sem, sub_sem,
):
    s = lax.axis_index("sub")
    g = lax.axis_index("grp")
    face = b_hbm.shape[0]
    nc = basis_hbm.shape[0]
    goals = b_hbm.shape[1]
    last_s = n_sub - 1
    at_end = s == last_s
    next_s = lax.rem(s + 1, n_sub)
    next_g = lax.rem(g + jnp.where(at_end, 1, 0), n_grp)
    prev_s = lax.rem(s + n_sub - 1, n_sub)
    prev_g = lax.rem(g + jnp.where(s == 0, n_grp - 1, 0), n_grp)
    above_g = lax.rem(g + 1, n_grp)
    below_g = lax.rem(g + n_grp - 1, n_grp)
    has_next = jnp.where(jnp.logical_and(at_end, g == n_grp - 1), 0.0, 1.0).astype(F32)
    has_prev = jnp.where(jnp.logical_and(s == 0, g == 0), 0.0, 1.0).astype(F32)
    nxt = {"sub": next_s, "grp": next_g}
    prv = {"sub": prev_s, "grp": prev_g}

    def local(src, dst, i):
        return pltpu.make_async_copy(src, dst, load_sem.at[i])

    loads = [
        local(b_hbm, res.at[pl.ds(0, face)], 0),
        local(occ_hbm, occ_v, 1),
        local(w_hbm, own_par.at[pl.ds(nc, 1)], 2),
        local(basis_hbm, own_par.at[pl.ds(0, nc)], 3),
        local(inv_hbm, inv.at[0], 4),
        local(s_hbm, blocks, 5),
    ]
    for copy in loads:
        copy.start()

    barrier = pltpu.get_barrier_semaphore()

    def greet(sub, grp):
        pl.semaphore_signal(barrier, inc=1, device_id={"sub": sub, "grp": grp}, device_id_type=MESH)

    def greet_sub(j, carry):
        greet(lax.rem(s + j, n_sub), g)
        return carry

    def greet_grp(j, carry):
        greet(s, lax.rem(g + j, n_grp))
        return carry

    lax.fori_loop(1, n_sub, greet_sub, 0)
    lax.fori_loop(1, n_grp, greet_grp, 0)

    @pl.when(s != last_s)
    def _():
        greet(last_s, below_g)

    @pl.when(at_end)
    def _():
        def greet_above(j, carry):
            greet(j, above_g)
            return carry

        lax.fori_loop(0, last_s, greet_above, 0)

    def remote(src, dst, send, recv, sub, grp):
        return pltpu.make_async_remote_copy(
            src_ref=src, dst_ref=dst, send_sem=send, recv_sem=recv,
            device_id={"sub": sub, "grp": grp}, device_id_type=MESH,
        )

    def take(ref, sem):
        pltpu.make_async_copy(ref, ref, sem).wait()

    def gather_coarse(k, value):
        coarse_src[k] = value
        coarse_all[k, 0, pl.ds(s, 1)] = value[None]

        def one(j, carry):
            remote(coarse_src.at[k], coarse_all.at[k, 0, s], send_sem.at[0, k], all_sem.at[k], lax.rem(s + j, n_sub), g).start()
            return carry

        lax.fori_loop(1, n_sub, one, 0)
        remote(coarse_src.at[k], coarse_all.at[k, 1, s], send_sem.at[1, k], far_sem.at[k], last_s, below_g).start()

    def solve_coarse(k):
        take(coarse_all.at[k, 0, pl.ds(0, n_sub - 1)], all_sem.at[k])

        @pl.when(at_end)
        def _():
            take(coarse_all.at[k, 1], far_sem.at[k])

        own = coarse_all[k, 0].reshape(n_sub * nc, goals)
        beside = coarse_all[k, jnp.where(at_end, 1, 0)].reshape(n_sub * nc, goals)
        dot = functools.partial(jnp.dot, precision=lax.Precision.HIGHEST, preferred_element_type=F32)
        return dot(inv[0], own), dot(inv[1], beside)

    loads[0].wait()
    loads[1].wait()
    loads[2].wait()
    loads[3].wait()
    own_par[pl.ds(nc + 1, 1)] = occ_v[...].astype(F32)

    def split_rows(rows):
        high, low = split(rows)
        return jnp.concatenate([high, low], axis=0)

    own_basis = split_rows(own_par[0:nc])
    coarse = jnp.zeros((2 * nc, 2 * goals), F32)
    for row in range(0, face, CH):
        high, low = split(res[pl.ds(row, CH)])
        half_b[pl.ds(row, CH)] = high
        coarse += jnp.dot(own_basis[:, row:row + CH], jnp.concatenate([high, low], axis=1), preferred_element_type=F32)

    def unsplit(value, rows):
        both = value[:, :goals] + value[:, goals:]
        return both[:rows] + both[rows:]

    first_coarse = unsplit(coarse, nc)
    pl.semaphore_wait(barrier, (n_sub - 1) + (n_grp - 1) + jnp.where(at_end, n_sub - 1, 1))
    gather_coarse(0, first_coarse)
    remote(own_par, next_par, send_sem.at[2, 0], par_sem, prev_s, prev_g).start()
    loads[4].wait()
    remote(inv.at[0], inv.at[1], send_sem.at[3, 0], inv_sem, prev_s, prev_g).start()
    remote(half_b, held, send_sem.at[4, 0], half_sem, prev_s, prev_g).start()

    def prepare(base, params):
        high, low = split(params[0:nc])
        quad = jnp.concatenate([high, high, low, low], axis=0).astype(F32)
        for col in range(0, face, 128):
            span = pl.ds(base + col, 128)
            basis_t[span] = jnp.transpose(quad[:, col:col + 128]).astype(BF16)
            weight[span] = jnp.transpose(jnp.broadcast_to(params[nc:nc + 1, col:col + 128], (128, 128)))
            free[span] = jnp.transpose(jnp.broadcast_to(params[nc + 1:nc + 2, col:col + 128], (128, 128)))

    def through(base, params, which):
        rows = split_rows(params[0:nc] * params[nc + 1:nc + 2])
        for col in range(0, 2 * face, CH):
            out = jnp.dot(rows, blocks[pl.ds(base, face), pl.ds(col, CH)], preferred_element_type=F32)
            high, low = split(out[:nc] + out[nc:])
            qmat[which, 0:nc, pl.ds(col, CH)] = high
            qmat[which, nc:2 * nc, pl.ds(col, CH)] = low

    params = own_par[...]
    prepare(0, params)
    basis_n[...] = split_rows(params[0:nc] * (1.0 - params[nc + 1:nc + 2]))
    loads[5].wait()
    through(0, params, 0)
    take(next_par, par_sem)
    params = next_par[...] * has_next
    prepare(face, params)
    through(face, params, 1)
    take(inv.at[1], inv_sem)

    def stage_spread(which, value):
        high, low = split(value)
        spread_rhs[which] = jnp.concatenate([high, low, high, low], axis=0)

    def build(span, which, r):
        z = weight[span] * r + jnp.dot(basis_t[span], spread_rhs[which], preferred_element_type=F32)
        fz = free[span] * z
        high, low = split(fz)
        masked[span, 0:goals] = high
        masked[span, goals:2 * goals] = low
        zed[span] = z
        return z, fz

    zero8 = jnp.zeros((8, goals), F32)
    solved, solved_next = solve_coarse(0)
    stage_spread(0, solved)
    stage_spread(1, solved_next)

    def leftover(span, rest):
        high, low = split(rest)
        prob[span, 0:goals] = high
        prob[span, goals:2 * goals] = low

    def first_own(i, carry):
        gamma, delta = carry
        span = place(i * CH)
        r = res[span]
        z, fz = build(span, 0, r)
        rest = z - fz
        leftover(span, rest)
        return gamma + folded(r * z), delta + folded(rest * z)

    gamma, delta = lax.fori_loop(0, face // CH, first_own, (zero8, zero8))
    eps = zero8
    take(held, half_sem)

    def first_next(i, carry):
        span = place(face + i * CH)
        r = held[place(i * CH)].astype(F32) * has_next
        res[span] = r
        build(span, 1, r)
        return carry

    lax.fori_loop(0, face // CH, first_next, 0)

    gamma_old = p_ap = None
    drift = drift_next = None
    for k in range(ITERS):
        more = k + 1 < ITERS
        if more:
            m_all = masked[...]
            part = jnp.dot(qmat[0], m_all, preferred_element_type=F32)
            kap = jnp.dot(qmat[1], m_all, preferred_element_type=F32)
            part += jnp.dot(basis_n[...], prob[...], preferred_element_type=F32)
            kap_src[k] = unsplit(kap, nc)
            remote(kap_src.at[k], kap_in.at[k], send_sem.at[5, k], kap_sem.at[k], next_s, next_g).start()
            part = unsplit(part, nc)

        def rows_of(row, acc):
            span = place(row)
            y = jnp.dot(blocks[span], masked[...], preferred_element_type=F32)
            y = y[:, :goals] + y[:, goals:]
            prod[span] = y
            leave[k, span] = y.astype(BF16)
            return acc + folded(free[span] * zed[span] * y)

        def pair(i, acc):
            acc = rows_of(face + i * CH, acc)
            remote(
                leave.at[k, place(face + i * CH)], arrive.at[k, place(i * CH)],
                send_sem.at[6, k], bulk_sem.at[k, 0], next_s, next_g,
            ).start()
            acc = rows_of(i * CH, acc)
            if more:
                remote(
                    leave.at[k, place(i * CH)], arrive.at[k, place(face + i * CH)],
                    send_sem.at[7, k], bulk_sem.at[k, 1], prev_s, prev_g,
                ).start()
            return acc

        delta = lax.fori_loop(0, face // CH, pair, delta)
        dots = [jnp.sum(v, axis=0, keepdims=True) for v in (gamma, delta, eps)]
        dots = jnp.concatenate(dots + [jnp.zeros((1, goals), F32)], axis=0)
        dot_src[k] = dots
        dot_grp[k, pl.ds(g, 1)] = dots[None]

        def to_grp(j, carry):
            remote(dot_src.at[k], dot_grp.at[k, g], send_sem.at[8, k], grp_sem.at[k], s, lax.rem(g + j, n_grp)).start()
            return carry

        lax.fori_loop(1, n_grp, to_grp, 0)
        if more:
            take(kap_in.at[k], kap_sem.at[k])
            gather_coarse(k + 1, part + kap_in[k] * has_prev)
        take(dot_grp.at[k, pl.ds(0, n_grp - 1)], grp_sem.at[k])
        dots = jnp.sum(dot_grp[k], axis=0)
        dot_mid[k] = dots
        dot_sub[k, pl.ds(s, 1)] = dots[None]

        def to_sub(j, carry):
            remote(dot_mid.at[k], dot_sub.at[k, s], send_sem.at[9, k], sub_sem.at[k], lax.rem(s + j, n_sub), g).start()
            return carry

        lax.fori_loop(1, n_sub, to_sub, 0)
        if more:
            moved, moved_next = solve_coarse(k + 1)
        take(arrive.at[k, pl.ds(0, face)], bulk_sem.at[k, 0])
        if more:
            take(arrive.at[k, pl.ds(face, face)], bulk_sem.at[k, 1])
        take(dot_sub.at[k, pl.ds(0, n_sub - 1)], sub_sem.at[k])
        dots = jnp.sum(dot_sub[k], axis=0)
        gamma_now, delta_now, eps_now = dots[0:1], dots[1:2], dots[2:3]
        if k == 0:
            p_ap = delta_now
            beta = None
        else:
            beta = gamma_now / gamma_old
            p_ap = delta_now + beta * (2.0 * eps_now + beta * p_ap)
        alpha = gamma_now / p_ap
        gamma_old = gamma_now
        if more:
            drift = moved if k == 0 else moved + beta * drift
            drift_next = moved_next if k == 0 else moved_next + beta * drift_next
            solved = solved - alpha * drift
            solved_next = solved_next - alpha * drift_next
            stage_spread(0, solved)
            stage_spread(1, solved_next)

        def advance(span, came):
            fr = free[span]
            w = fr * (prod[span] + came) + (1.0 - fr) * zed[span]
            sr = w if k == 0 else w + beta * srch[span]
            return sr, res[span] - alpha * sr

        def own_rows(i, carry):
            gamma, delta, eps = carry
            span = place(i * CH)
            sr, r = advance(span, arrive[k, span].astype(F32) * has_prev)
            d = zed[span] if k == 0 else zed[span] + beta * direc[span]
            x = alpha * d if k == 0 else x_ref[span] + alpha * d
            x_ref[span] = x
            if not more:
                r_ref[span] = r
                return carry
            direc[span] = d
            srch[span] = sr
            res[span] = r
            z, fz = build(span, 0, r)
            rest = z - fz
            if k + 2 < ITERS:
                leftover(span, rest)
            return gamma + folded(r * z), delta + folded(rest * z), eps + folded(z * sr)

        gamma, delta, eps = lax.fori_loop(0, face // CH, own_rows, (zero8, zero8, zero8))
        if more:
            def next_rows(i, carry):
                span = place(face + i * CH)
                sr, r = advance(span, arrive[k, span].astype(F32))
                srch[span] = sr
                res[span] = r
                build(span, 1, r)
                return carry

            lax.fori_loop(0, face // CH, next_rows, 0)

    for k in range(ITERS):
        take(coarse_all.at[k, 0, pl.ds(0, n_sub - 1)], send_sem.at[0, k])
        take(coarse_src.at[k], send_sem.at[1, k])
        take(leave.at[k, pl.ds(face, face)], send_sem.at[6, k])
        if k + 1 < ITERS:
            take(leave.at[k, pl.ds(0, face)], send_sem.at[7, k])
            take(kap_src.at[k], send_sem.at[5, k])
        take(dot_grp.at[k, pl.ds(0, n_grp - 1)], send_sem.at[8, k])
        take(dot_sub.at[k, pl.ds(0, n_sub - 1)], send_sem.at[9, k])
    take(own_par, send_sem.at[2, 0])
    take(inv.at[0], send_sem.at[3, 0])
    take(half_b, send_sem.at[4, 0])


def solution(mesh):
    n_sub, n_grp = mesh.shape["sub"], mesh.shape["grp"]

    def local(right_side, schur_blocks, occupancy, precond_weights, coarse_basis, coarse_inverse):
        face, goals = right_side.shape[2:]
        nc = coarse_basis.shape[2]
        both = 2 * face
        dma = pltpu.SemaphoreType.DMA
        out = jax.ShapeDtypeStruct((face, goals), F32)
        x, r = pl.pallas_call(
            functools.partial(kernel, n_sub, n_grp),
            out_shape=(out, out),
            in_specs=[pl.BlockSpec(memory_space=pl.ANY)] * 6,
            out_specs=[pl.BlockSpec(memory_space=pltpu.VMEM)] * 2,
            scratch_shapes=[
                pltpu.VMEM((both, both), BF16),
                pltpu.VMEM((both, goals), F32),
                pltpu.VMEM((both, goals), F32),
                pltpu.VMEM((both, goals), F32),
                pltpu.VMEM((both, goals), F32),
                pltpu.VMEM((both, goals), F32),
                pltpu.VMEM((both, goals), F32),
                pltpu.VMEM((both, 2 * goals), BF16),
                pltpu.VMEM((face, goals), BF16),
                pltpu.VMEM((ITERS, both, goals), BF16),
                pltpu.VMEM((ITERS, both, goals), BF16),
                pltpu.VMEM((face, goals), BF16),
                pltpu.VMEM((nc + 8, face), F32),
                pltpu.VMEM((nc + 8, face), F32),
                pltpu.VMEM((1, face), jnp.int32),
                pltpu.VMEM((2, nc, n_sub * nc), F32),
                pltpu.VMEM((both, 4 * nc), BF16),
                pltpu.VMEM((2, 4 * nc, goals), BF16),
                pltpu.VMEM((face, 2 * goals), BF16),
                pltpu.VMEM((2, 2 * nc, both), BF16),
                pltpu.VMEM((2 * nc, face), BF16),
                pltpu.VMEM((face, goals), F32),
                pltpu.VMEM((ITERS, nc, goals), F32),
                pltpu.VMEM((ITERS, 2, n_sub, nc, goals), F32),
                pltpu.VMEM((ITERS, nc, goals), F32),
                pltpu.VMEM((ITERS, nc, goals), F32),
                pltpu.VMEM((ITERS, 4, goals), F32),
                pltpu.VMEM((ITERS, n_grp, 4, goals), F32),
                pltpu.VMEM((ITERS, 4, goals), F32),
                pltpu.VMEM((ITERS, n_sub, 4, goals), F32),
                dma((6,)),
                dma((10, ITERS)),
                dma,
                dma,
                dma,
                dma((ITERS, 2)),
                dma((ITERS,)),
                dma((ITERS,)),
                dma((ITERS,)),
                dma((ITERS,)),
                dma((ITERS,)),
            ],
            compiler_params=pltpu.CompilerParams(
                collective_id=0, has_side_effects=True, vmem_limit_bytes=48 << 20
            ),
        )(right_side[0, 0], schur_blocks[0, 0], occupancy[0], precond_weights[0], coarse_basis[0, 0], coarse_inverse[0])
        return x[None, None], r[None, None]

    return jax.shard_map(
        local,
        mesh=mesh,
        in_specs=(
            P("grp", "sub", None, None),
            P("grp", "sub", None, None),
            P("grp", "sub", None),
            P("grp", "sub", None),
            P("grp", "sub", None, None),
            P("grp", "sub", None),
        ),
        out_specs=(P("grp", "sub", None, None), P("grp", "sub", None, None)),
        check_vma=False,
    )
```

```python
import functools

import jax
import jax.numpy as jnp
from jax import lax
from jax.experimental import pallas as pl
from jax.experimental.pallas import tpu as pltpu
from jax.sharding import PartitionSpec as P

ITERS = 3
MESH = pl.DeviceIdType.MESH
F32 = jnp.float32
BF16 = jnp.bfloat16
CH = 256
PLANE = 8
CORES = 2
ROW = 4


def split(value):
    high = value.astype(BF16)
    return high, (value - high.astype(F32)).astype(BF16)


def folded(value):
    return jnp.sum(value.reshape(value.shape[0] // 8, 8, value.shape[1]), axis=0)


def place(row):
    return pl.ds(pl.multiple_of(row, CH), CH)


def kernel(
    n_sub, n_grp,
    b_hbm, s_hbm, occ_hbm, w_hbm, basis_hbm, inv_hbm,
    x_out, r_out,
    x_ref, r_ref,
    blocks, res, zed, srch, prod, weight, free, masked, held, arrive, leave, half_b,
    own_par, next_par, occ_v, weight_v, inv, basis_t, spread_rhs, prob, qmat, basis_n, basis_f, alone, qsum, qcol, solved_rhs, direc,
    coarse_src, coarse_all, kap_src, kap_in, dot_src, dot_grp, dot_mid, dot_sub,
    load_sem, send_sem, par_sem, half_sem, inv_sem, bulk_sem, kap_sem, all_sem, far_sem, grp_sem, sub_sem, out_sem, swap_sem,
):
    s = lax.axis_index("sub")
    g = lax.axis_index("grp")
    face = b_hbm.shape[0]
    nc = basis_hbm.shape[0]
    goals = b_hbm.shape[1]
    last_s = n_sub - 1
    at_end = s == last_s
    next_s = lax.rem(s + 1, n_sub)
    next_g = lax.rem(g + jnp.where(at_end, 1, 0), n_grp)
    prev_s = lax.rem(s + n_sub - 1, n_sub)
    prev_g = lax.rem(g + jnp.where(s == 0, n_grp - 1, 0), n_grp)
    above_g = lax.rem(g + 1, n_grp)
    below_g = lax.rem(g + n_grp - 1, n_grp)
    has_next = jnp.where(jnp.logical_and(at_end, g == n_grp - 1), 0.0, 1.0).astype(F32)
    has_prev = jnp.where(jnp.logical_and(s == 0, g == 0), 0.0, 1.0).astype(F32)
    nxt = {"sub": next_s, "grp": next_g}
    prv = {"sub": prev_s, "grp": prev_g}

    def local(src, dst, i):
        return pltpu.make_async_copy(src, dst, load_sem.at[i])

    loads = [
        local(b_hbm, res.at[pl.ds(0, face)], 0),
        local(occ_hbm, occ_v, 1),
        local(w_hbm, weight_v, 2),
        local(basis_hbm, own_par.at[pl.ds(0, nc)], 3),
        local(inv_hbm, inv.at[0], 4),
        local(s_hbm, blocks, 5),
    ]
    for copy in loads:
        copy.start()

    barrier = pltpu.get_barrier_semaphore()

    def greet(sub, grp):
        pl.semaphore_signal(barrier, inc=1, device_id={"sub": sub, "grp": grp}, device_id_type=MESH)

    def greet_sub(j, carry):
        greet(lax.rem(s + j, n_sub), g)
        return carry

    corner = g // ROW * ROW
    n_near = PLANE * ROW
    n_far = n_sub * n_grp // n_near
    core = lax.rem(s, PLANE)
    my_near = core * ROW + g - corner
    my_far = s // PLANE * (n_grp // ROW) + g // ROW

    def near(j):
        i = lax.rem(my_near + j, n_near)
        return s - core + i // ROW, corner + lax.rem(i, ROW)

    def far(j):
        i = lax.rem(my_far + j, n_far)
        return i // (n_grp // ROW) * PLANE + core, lax.rem(i, n_grp // ROW) * ROW + g - corner

    def greet_near(j, carry):
        greet(*near(j))
        return carry

    def greet_far(j, carry):
        greet(*far(j))
        return carry

    lax.fori_loop(1, n_sub, greet_sub, 0)
    lax.fori_loop(1, n_near, greet_near, 0)
    lax.fori_loop(1, n_far, greet_far, 0)

    greet(last_s, below_g)

    @pl.when(at_end)
    def _():
        def greet_above(j, carry):
            greet(j, above_g)
            return carry

        lax.fori_loop(0, n_sub, greet_above, 0)

    def remote(src, dst, send, recv, sub, grp):
        return pltpu.make_async_remote_copy(
            src_ref=src, dst_ref=dst, send_sem=send, recv_sem=recv,
            device_id={"sub": sub, "grp": grp}, device_id_type=MESH,
        )

    def take(ref, sem):
        pltpu.make_async_copy(ref, ref, sem).wait()

    chips = n_sub // CORES
    side = lax.rem(s, CORES)
    chip = s // CORES
    mine = pl.ds(side * chips, chips)

    def gather_coarse(k, value):
        coarse_src[k] = value
        coarse_all[k, 0, pl.ds(side * chips + chip, 1)] = value[None]

        def one(j, carry):
            remote(
                coarse_src.at[k], coarse_all.at[k, 0, side * chips + chip], send_sem.at[0, k], all_sem.at[k],
                lax.rem(chip + j, chips) * CORES + side, g,
            ).start()
            return carry

        lax.fori_loop(1, chips, one, 0)
        remote(
            coarse_src.at[k], coarse_all.at[k, 1, side * chips + chip], send_sem.at[1, k], far_sem.at[k], last_s, below_g
        ).start()

    def swap_coarse(k):
        take(coarse_all.at[k, 0, pl.ds(0, chips - 1)], all_sem.at[k])
        remote(
            coarse_all.at[k, 0, mine], coarse_all.at[k, 0, mine], send_sem.at[10, k], swap_sem.at[k], s + 1 - 2 * side, g
        ).start()

    def solve_coarse(k):
        take(coarse_all.at[k, 0, mine], swap_sem.at[k])

        @pl.when(at_end)
        def _():
            take(coarse_all.at[k, 1], far_sem.at[k])

        def in_order(blocks_of):
            parts = [blocks_of[i * chips:(i + 1) * chips] for i in range(CORES)]
            return jnp.stack(parts, axis=1).reshape(n_sub * nc, goals)

        own = in_order(coarse_all[k, 0])
        beside = in_order(coarse_all[k, jnp.where(at_end, 1, 0)])
        dot = functools.partial(jnp.dot, precision=lax.Precision.HIGHEST, preferred_element_type=F32)
        return dot(inv[0], own), dot(inv[1], beside)

    loads[0].wait()
    loads[1].wait()
    loads[2].wait()
    loads[3].wait()
    own_par[pl.ds(nc, 8)] = jnp.concatenate([weight_v[...], occ_v[...].astype(F32), jnp.zeros((6, face), F32)], axis=0)

    def split_rows(rows):
        high, low = split(rows)
        return jnp.concatenate([high, low], axis=0)

    own_basis = split_rows(own_par[0:nc])
    coarse = jnp.zeros((2 * nc, 2 * goals), F32)
    for row in range(0, face, CH):
        high, low = split(res[pl.ds(row, CH)])
        half_b[pl.ds(row, CH)] = high
        coarse += jnp.dot(own_basis[:, row:row + CH], jnp.concatenate([high, low], axis=1), preferred_element_type=F32)

    def unsplit(value, rows):
        both = value[:, :goals] + value[:, goals:]
        return both[:rows] + both[rows:]

    first_coarse = unsplit(coarse, nc)

    line = lax.broadcasted_iota(jnp.int32, (8 * nc, 2 * goals), 0)
    lane = lax.broadcasted_iota(jnp.int32, (8 * nc, 2 * goals), 1)
    is_weight = jnp.logical_and(line >= 6 * nc, jnp.logical_and(line < 6 * nc + 3, lane < goals))
    is_free = jnp.logical_and(line == 6 * nc + 3, lane >= goals)
    pick = jnp.logical_or(is_weight, is_free).astype(F32).astype(BF16)

    def prepare(base, params):
        basis, wrow, frow = params[0:nc], params[nc:nc + 1], params[nc + 1:nc + 2]
        high, low = split(basis)
        fhigh, flow = split(basis * frow)
        whigh = wrow.astype(BF16).astype(F32)
        wmid = (wrow - whigh).astype(BF16).astype(F32)
        rest = [whigh, wmid, wrow - whigh - wmid, frow]
        tall = [high, high, low, low, fhigh, flow]
        tall = jnp.concatenate([t.astype(F32) for t in tall] + rest + [jnp.zeros((2 * nc - 4, face), F32)], axis=0)
        for col in range(0, face, 128):
            span = pl.ds(base + col, 128)
            cols = jnp.transpose(tall[:, col:col + 128]).astype(BF16)
            basis_t[span] = cols
            both = jnp.dot(cols, pick, preferred_element_type=F32)
            weight[span] = both[:, :goals]
            free[span] = both[:, goals:]
            some, none = cols[:, 4 * nc:6 * nc], jnp.zeros((128, 2 * nc), BF16)
            basis_f[span] = jnp.concatenate([some, none] if base == 0 else [none, some], axis=1)

    params = own_par[...]
    prepare(0, params)
    basis_n[...] = split_rows(params[0:nc] * (1.0 - params[nc + 1:nc + 2]))

    def weighted(i, span):
        high, low = split(free[span] * (weight[span] * res[span]))
        here = place(i * CH)
        alone[here, 0:goals] = high
        alone[here, goals:2 * goals] = low

    def weighted_own(i, carry):
        weighted(i, place(i * CH))
        return carry

    lax.fori_loop(0, face // CH, weighted_own, 0)
    loads[5].wait()

    def half_own(i, carry):
        span = place(i * CH)
        left = blocks[span, 0:face]
        y = jnp.dot(left, alone[...], preferred_element_type=F32)
        prod[span] = y[:, :goals] + y[:, goals:]
        qsum[span] = jnp.dot(left, basis_f[0:face], preferred_element_type=F32)
        return carry

    lax.fori_loop(0, 2 * face // CH, half_own, 0)
    pl.semaphore_wait(barrier, (n_sub - 1) + (n_near - 1) + (n_far - 1) + jnp.where(at_end, n_sub + 1, 1))
    remote(own_par, next_par, send_sem.at[2, 0], par_sem, prev_s, prev_g).start()
    loads[4].wait()
    remote(inv.at[0], inv.at[1], send_sem.at[3, 0], inv_sem, prev_s, prev_g).start()
    remote(half_b, held, send_sem.at[4, 0], half_sem, prev_s, prev_g).start()
    gather_coarse(0, first_coarse)
    take(next_par, par_sem)
    prepare(face, next_par[...] * has_next)

    def through(i, carry):
        span = place(i * CH)
        out = qsum[span] + jnp.dot(blocks[span, face:2 * face], basis_f[face:2 * face], preferred_element_type=F32)
        out = jnp.transpose(out)
        high, low = split(jnp.concatenate([out[0:nc] + out[nc:2 * nc], out[2 * nc:3 * nc] + out[3 * nc:]], axis=0))
        qmat[:, span] = jnp.concatenate([high, low], axis=0)
        high, low = high.astype(F32), low.astype(F32)
        qcol[span] = jnp.transpose(jnp.concatenate([high, high, low, low], axis=0)).astype(BF16)
        return carry

    lax.fori_loop(0, 2 * face // CH, through, 0)
    swap_coarse(0)
    take(inv.at[1], inv_sem)

    def stage_spread(which, value):
        high, low = split(value)
        spread_rhs[which] = jnp.concatenate([high, low, high, low, jnp.zeros((4 * nc, goals), BF16)], axis=0)

    def build(span, which, r):
        z = weight[span] * r + jnp.dot(basis_t[span], spread_rhs[which], preferred_element_type=F32)
        fz = free[span] * z
        high, low = split(fz)
        masked[span, 0:goals] = high
        masked[span, goals:2 * goals] = low
        zed[span] = z
        return z, fz

    zero8 = jnp.zeros((8, goals), F32)
    solved, solved_next = solve_coarse(0)
    stage_spread(0, solved)
    stage_spread(1, solved_next)
    high, low = split(jnp.concatenate([solved, solved_next], axis=0))
    solved_rhs[...] = jnp.concatenate([high, low, high, low], axis=0)

    def leftover(span, rest):
        high, low = split(rest)
        prob[span, 0:goals] = high
        prob[span, goals:2 * goals] = low

    def first_own(i, carry):
        gamma, delta = carry
        span = place(i * CH)
        r = res[span]
        z, fz = build(span, 0, r)
        rest = z - fz
        leftover(span, rest)
        return gamma + folded(r * z), delta + folded(rest * z)

    gamma, delta = lax.fori_loop(0, face // CH, first_own, (zero8, zero8))
    eps = zero8
    take(held, half_sem)

    def first_next(i, carry):
        span = place(face + i * CH)
        r = held[place(i * CH)].astype(F32) * has_next
        res[span] = r
        build(span, 1, r)
        weighted(i, span)
        return carry

    lax.fori_loop(0, face // CH, first_next, 0)

    gamma_old = p_ap = None
    drift = drift_next = None
    for k in range(ITERS):
        more = k + 1 < ITERS
        if more:
            out = jnp.dot(qmat[...], masked[...], preferred_element_type=F32)
            part = jnp.dot(basis_n[...], prob[...], preferred_element_type=F32)
            out = out[:, :goals] + out[:, goals:]
            out = out[:2 * nc] + out[2 * nc:]
            kap_src[k] = out[nc:]
            remote(kap_src.at[k], kap_in.at[k], send_sem.at[5, k], kap_sem.at[k], next_s, next_g).start()
            part = unsplit(part, nc) + out[:nc]

        def rows_of(row, acc):
            span = place(row)
            if k == 0:
                y = jnp.dot(blocks[span, face:2 * face], alone[...], preferred_element_type=F32)
                y = prod[span] + y[:, :goals] + y[:, goals:]
                y += jnp.dot(qcol[span], solved_rhs[...], preferred_element_type=F32)
            else:
                y = jnp.dot(blocks[span], masked[...], preferred_element_type=F32)
                y = y[:, :goals] + y[:, goals:]
            prod[span] = y
            leave[k, span] = y.astype(BF16)
            return acc + folded(free[span] * zed[span] * y)

        def pair(i, acc):
            acc = rows_of(face + i * CH, acc)
            remote(
                leave.at[k, place(face + i * CH)], arrive.at[k, place(i * CH)],
                send_sem.at[6, k], bulk_sem.at[k, 0], next_s, next_g,
            ).start()
            acc = rows_of(i * CH, acc)
            if more:
                remote(
                    leave.at[k, place(i * CH)], arrive.at[k, place(face + i * CH)],
                    send_sem.at[7, k], bulk_sem.at[k, 1], prev_s, prev_g,
                ).start()
            return acc

        delta = lax.fori_loop(0, face // CH, pair, delta)
        dots = [jnp.sum(v, axis=0, keepdims=True) for v in (gamma, delta, eps)]
        dots = jnp.concatenate(dots + [jnp.zeros((1, goals), F32)], axis=0)
        dot_src[k] = dots
        dot_grp[k, pl.ds(my_near, 1)] = dots[None]

        def to_grp(j, carry):
            remote(dot_src.at[k], dot_grp.at[k, my_near], send_sem.at[8, k], grp_sem.at[k], *near(j)).start()
            return carry

        lax.fori_loop(1, n_near, to_grp, 0)
        if more:
            take(kap_in.at[k], kap_sem.at[k])
            gather_coarse(k + 1, part + kap_in[k] * has_prev)
        take(dot_grp.at[k, pl.ds(0, n_near - 1)], grp_sem.at[k])
        dots = jnp.sum(dot_grp[k], axis=0)
        dot_mid[k] = dots
        dot_sub[k, pl.ds(my_far, 1)] = dots[None]

        def to_sub(j, carry):
            remote(dot_mid.at[k], dot_sub.at[k, my_far], send_sem.at[9, k], sub_sem.at[k], *far(j)).start()
            return carry

        lax.fori_loop(1, n_far, to_sub, 0)
        if more:
            swap_coarse(k + 1)
            moved, moved_next = solve_coarse(k + 1)
        take(arrive.at[k, pl.ds(0, face)], bulk_sem.at[k, 0])
        if more:
            take(arrive.at[k, pl.ds(face, face)], bulk_sem.at[k, 1])

        def apply(i, carry):
            span = place(i * CH)
            fr = free[span]
            came = arrive[k, span].astype(F32) * jnp.where(i < face // CH, has_prev, 1.0)
            prod[span] = fr * (prod[span] + came) + (1.0 - fr) * zed[span]
            return carry

        lax.fori_loop(0, (2 if more else 1) * face // CH, apply, 0)
        take(dot_sub.at[k, pl.ds(0, n_far - 1)], sub_sem.at[k])
        dots = jnp.sum(dot_sub[k], axis=0)
        gamma_now, delta_now, eps_now = dots[0:1], dots[1:2], dots[2:3]
        if k == 0:
            p_ap = delta_now
            beta = None
        else:
            beta = gamma_now / gamma_old
            p_ap = delta_now + beta * (2.0 * eps_now + beta * p_ap)
        alpha = gamma_now / p_ap
        gamma_old = gamma_now
        if more:
            drift = moved if k == 0 else moved + beta * drift
            drift_next = moved_next if k == 0 else moved_next + beta * drift_next
            solved = solved - alpha * drift
            solved_next = solved_next - alpha * drift_next
            stage_spread(0, solved)
            stage_spread(1, solved_next)

        def advance(span):
            sr = prod[span] if k == 0 else prod[span] + beta * srch[span]
            return sr, res[span] - alpha * sr

        def own_rows(i, carry):
            gamma, delta, eps = carry
            span = place(i * CH)
            sr, r = advance(span)
            d = zed[span] if k == 0 else zed[span] + beta * direc[span]
            x = alpha * d if k == 0 else x_ref[span] + alpha * d
            x_ref[span] = x
            if not more:
                r_ref[span] = r
                pltpu.make_async_copy(x_ref.at[span], x_out.at[span], out_sem.at[0, i]).start()
                pltpu.make_async_copy(r_ref.at[span], r_out.at[span], out_sem.at[1, i]).start()
                return carry
            direc[span] = d
            srch[span] = sr
            res[span] = r
            z, fz = build(span, 0, r)
            rest = z - fz
            if k + 2 < ITERS:
                leftover(span, rest)
            return gamma + folded(r * z), delta + folded(rest * z), eps + folded(z * sr)

        gamma, delta, eps = lax.fori_loop(0, face // CH, own_rows, (zero8, zero8, zero8))
        if more:
            def next_rows(i, carry):
                span = place(face + i * CH)
                sr, r = advance(span)
                srch[span] = sr
                res[span] = r
                build(span, 1, r)
                return carry

            lax.fori_loop(0, face // CH, next_rows, 0)

    for i in range(face // CH):
        pltpu.make_async_copy(x_ref.at[pl.ds(i * CH, CH)], x_out.at[pl.ds(i * CH, CH)], out_sem.at[0, i]).wait()
        pltpu.make_async_copy(r_ref.at[pl.ds(i * CH, CH)], r_out.at[pl.ds(i * CH, CH)], out_sem.at[1, i]).wait()
    for k in range(ITERS):
        take(coarse_all.at[k, 0, pl.ds(0, chips - 1)], send_sem.at[0, k])
        take(coarse_all.at[k, 0, mine], send_sem.at[10, k])
        take(coarse_src.at[k], send_sem.at[1, k])
        take(leave.at[k, pl.ds(face, face)], send_sem.at[6, k])
        if k + 1 < ITERS:
            take(leave.at[k, pl.ds(0, face)], send_sem.at[7, k])
            take(kap_src.at[k], send_sem.at[5, k])
        take(dot_grp.at[k, pl.ds(0, n_near - 1)], send_sem.at[8, k])
        take(dot_sub.at[k, pl.ds(0, n_far - 1)], send_sem.at[9, k])
    take(own_par, send_sem.at[2, 0])
    take(inv.at[0], send_sem.at[3, 0])
    take(half_b, send_sem.at[4, 0])


def ship(x_in, r_in, x_out, r_out, held, sem):
    moves = []
    for which, (src, dst) in enumerate(((x_in, x_out), (r_in, r_out))):
        for i in range(src.shape[0] // CH):
            span = pl.ds(i * CH, CH)
            inward = pltpu.make_async_copy(src.at[span], held.at[which, span], sem.at[0, which, i])
            outward = pltpu.make_async_copy(held.at[which, span], dst.at[span], sem.at[1, which, i])
            inward.start()
            moves.append((inward, outward))
    for inward, outward in moves:
        inward.wait()
        outward.start()
    for inward, outward in moves:
        outward.wait()


def solution(mesh):
    n_sub, n_grp = mesh.shape["sub"], mesh.shape["grp"]

    def local(right_side, schur_blocks, occupancy, precond_weights, coarse_basis, coarse_inverse):
        face, goals = right_side.shape[2:]
        nc = coarse_basis.shape[2]
        both = 2 * face
        dma = pltpu.SemaphoreType.DMA
        out = jax.ShapeDtypeStruct((face, goals), F32)
        x, r = pl.pallas_call(
            functools.partial(kernel, n_sub, n_grp),
            out_shape=(out, out),
            in_specs=[pl.BlockSpec(memory_space=pl.ANY)] * 6,
            out_specs=[pl.BlockSpec(memory_space=pl.ANY)] * 2,
            scratch_shapes=[
                pltpu.VMEM((face, goals), F32),
                pltpu.VMEM((face, goals), F32),
                pltpu.VMEM((both, both), BF16),
                pltpu.VMEM((both, goals), F32),
                pltpu.VMEM((both, goals), F32),
                pltpu.VMEM((both, goals), F32),
                pltpu.VMEM((both, goals), F32),
                pltpu.VMEM((both, goals), F32),
                pltpu.VMEM((both, goals), F32),
                pltpu.VMEM((both, 2 * goals), BF16),
                pltpu.VMEM((face, goals), BF16),
                pltpu.VMEM((ITERS, both, goals), BF16),
                pltpu.VMEM((ITERS, both, goals), BF16),
                pltpu.VMEM((face, goals), BF16),
                pltpu.VMEM((nc + 8, face), F32),
                pltpu.VMEM((nc + 8, face), F32),
                pltpu.VMEM((1, face), jnp.int32),
                pltpu.VMEM((1, face), F32),
                pltpu.VMEM((2, nc, n_sub * nc), F32),
                pltpu.VMEM((both, 8 * nc), BF16),
                pltpu.VMEM((2, 8 * nc, goals), BF16),
                pltpu.VMEM((face, 2 * goals), BF16),
                pltpu.VMEM((4 * nc, both), BF16),
                pltpu.VMEM((2 * nc, face), BF16),
                pltpu.VMEM((both, 4 * nc), BF16),
                pltpu.VMEM((face, 2 * goals), BF16),
                pltpu.VMEM((both, 4 * nc), F32),
                pltpu.VMEM((both, 8 * nc), BF16),
                pltpu.VMEM((8 * nc, goals), BF16),
                pltpu.VMEM((face, goals), F32),
                pltpu.VMEM((ITERS, nc, goals), F32),
                pltpu.VMEM((ITERS, 2, n_sub, nc, goals), F32),
                pltpu.VMEM((ITERS, nc, goals), F32),
                pltpu.VMEM((ITERS, nc, goals), F32),
                pltpu.VMEM((ITERS, 4, goals), F32),
                pltpu.VMEM((ITERS, PLANE * ROW, 4, goals), F32),
                pltpu.VMEM((ITERS, 4, goals), F32),
                pltpu.VMEM((ITERS, n_sub * n_grp // (PLANE * ROW), 4, goals), F32),
                dma((6,)),
                dma((11, ITERS)),
                dma,
                dma,
                dma,
                dma((ITERS, 2)),
                dma((ITERS,)),
                dma((ITERS,)),
                dma((ITERS,)),
                dma((ITERS,)),
                dma((ITERS,)),
                dma((2, face // CH)),
                dma((ITERS,)),
            ],
            compiler_params=pltpu.CompilerParams(
                collective_id=0, has_side_effects=True, vmem_limit_bytes=60 << 20
            ),
        )(right_side[0, 0], schur_blocks[0, 0], occupancy[0], precond_weights[0], coarse_basis[0, 0], coarse_inverse[0])
        x, r = pl.pallas_call(
            ship,
            out_shape=(out, out),
            in_specs=[pl.BlockSpec(memory_space=pl.ANY)] * 2,
            out_specs=[pl.BlockSpec(memory_space=pl.ANY)] * 2,
            scratch_shapes=[pltpu.VMEM((2, face, goals), F32), dma((2, 2, face // CH))],
        )(x, r)
        return x[None, None], r[None, None]

    return jax.shard_map(
        local,
        mesh=mesh,
        in_specs=(
            P("grp", "sub", None, None),
            P("grp", "sub", None, None),
            P("grp", "sub", None),
            P("grp", "sub", None),
            P("grp", "sub", None, None),
            P("grp", "sub", None),
        ),
        out_specs=(P("grp", "sub", None, None), P("grp", "sub", None, None)),
        check_vma=False,
    )
```

```python
import functools

import jax
import jax.numpy as jnp
from jax import lax
from jax.experimental import pallas as pl
from jax.experimental.pallas import tpu as pltpu
from jax.sharding import PartitionSpec as P

ITERS = 3
MESH = pl.DeviceIdType.MESH
F32 = jnp.float32
BF16 = jnp.bfloat16
CH = 256
TALL = 512
PLANE = 8
CORES = 2
ROW = 4


def split(value):
    high = value.astype(BF16)
    return high, (value - high.astype(F32)).astype(BF16)


def folded(value):
    return jnp.sum(value.reshape(value.shape[0] // 8, 8, value.shape[1]), axis=0)


def place(row, size=CH):
    return pl.ds(pl.multiple_of(row, size), size)


def kernel(
    n_sub, n_grp,
    b_hbm, s_hbm, occ_hbm, w_hbm, basis_hbm, inv_hbm,
    x_out, r_out,
    x_ref, r_ref,
    blocks, res, zed, tee, vee, srch, prod, weight, free, masked, held, arrive, leave, half_b,
    own_par, next_par, occ_v, weight_v, inv, basis_t, spread_rhs, prob, qmat, basis_n, basis_f, alone, qsum, qcol, solved_rhs, direc,
    coarse_src, coarse_all, kap_src, kap_in, dot_src, dot_grp, dot_mid, dot_sub,
    load_sem, send_sem, par_sem, half_sem, inv_sem, bulk_sem, kap_sem, all_sem, far_sem, grp_sem, sub_sem, out_sem, swap_sem,
):
    s = lax.axis_index("sub")
    g = lax.axis_index("grp")
    face = b_hbm.shape[0]
    nc = basis_hbm.shape[0]
    goals = b_hbm.shape[1]
    last_s = n_sub - 1
    at_end = s == last_s
    next_s = lax.rem(s + 1, n_sub)
    next_g = lax.rem(g + jnp.where(at_end, 1, 0), n_grp)
    prev_s = lax.rem(s + n_sub - 1, n_sub)
    prev_g = lax.rem(g + jnp.where(s == 0, n_grp - 1, 0), n_grp)
    above_g = lax.rem(g + 1, n_grp)
    below_g = lax.rem(g + n_grp - 1, n_grp)
    has_next = jnp.where(jnp.logical_and(at_end, g == n_grp - 1), 0.0, 1.0).astype(F32)
    has_prev = jnp.where(jnp.logical_and(s == 0, g == 0), 0.0, 1.0).astype(F32)
    nxt = {"sub": next_s, "grp": next_g}
    prv = {"sub": prev_s, "grp": prev_g}

    def local(src, dst, i):
        return pltpu.make_async_copy(src, dst, load_sem.at[i])

    loads = [
        local(b_hbm, res.at[pl.ds(0, face)], 0),
        local(occ_hbm, occ_v, 1),
        local(w_hbm, weight_v, 2),
        local(basis_hbm, own_par.at[pl.ds(0, nc)], 3),
        local(inv_hbm, inv.at[0], 4),
        local(s_hbm, blocks, 5),
    ]
    for copy in loads:
        copy.start()

    barrier = pltpu.get_barrier_semaphore()

    def greet(sub, grp):
        pl.semaphore_signal(barrier, inc=1, device_id={"sub": sub, "grp": grp}, device_id_type=MESH)

    chips = n_sub // CORES
    side = lax.rem(s, CORES)
    chip = s // CORES
    mine = pl.ds(side * chips, chips)

    def greet_like(j, carry):
        greet(lax.rem(chip + j, chips) * CORES + side, g)
        return carry

    corner = g // ROW * ROW
    n_near = PLANE * ROW
    n_far = n_sub * n_grp // n_near
    core = lax.rem(s, PLANE)
    my_near = core * ROW + g - corner
    my_far = s // PLANE * (n_grp // ROW) + g // ROW

    def near(j):
        i = lax.rem(my_near + j, n_near)
        return s - core + i // ROW, corner + lax.rem(i, ROW)

    def far(j):
        i = lax.rem(my_far + j, n_far)
        return i // (n_grp // ROW) * PLANE + core, lax.rem(i, n_grp // ROW) * ROW + g - corner

    def greet_near(j, carry):
        greet(*near(j))
        return carry

    def greet_far(j, carry):
        greet(*far(j))
        return carry

    greet(prev_s, prev_g)
    greet(next_s, next_g)
    lax.fori_loop(1, chips, greet_like, 0)
    lax.fori_loop(1, n_near, greet_near, 0)
    lax.fori_loop(1, n_far, greet_far, 0)

    greet(last_s, below_g)

    @pl.when(at_end)
    def _():
        def greet_above(j, carry):
            greet(j, above_g)
            return carry

        lax.fori_loop(0, n_sub, greet_above, 0)

    def remote(src, dst, send, recv, sub, grp):
        return pltpu.make_async_remote_copy(
            src_ref=src, dst_ref=dst, send_sem=send, recv_sem=recv,
            device_id={"sub": sub, "grp": grp}, device_id_type=MESH,
        )

    def take(ref, sem):
        pltpu.make_async_copy(ref, ref, sem).wait()


    def gather_coarse(k, value):
        coarse_src[k] = value
        coarse_all[k, 0, pl.ds(side * chips + chip, 1)] = value[None]

        def one(j, carry):
            remote(
                coarse_src.at[k], coarse_all.at[k, 0, side * chips + chip], send_sem.at[0, k], all_sem.at[k],
                lax.rem(chip + j, chips) * CORES + side, g,
            ).start()
            return carry

        lax.fori_loop(1, chips, one, 0)
        remote(
            coarse_src.at[k], coarse_all.at[k, 1, side * chips + chip], send_sem.at[1, k], far_sem.at[k], last_s, below_g
        ).start()

    def swap_coarse(k):
        take(coarse_all.at[k, 0, pl.ds(0, chips - 1)], all_sem.at[k])
        remote(
            coarse_all.at[k, 0, mine], coarse_all.at[k, 0, mine], send_sem.at[10, k], swap_sem.at[k], s + 1 - 2 * side, g
        ).start()

    def solve_coarse(k):
        take(coarse_all.at[k, 0, mine], swap_sem.at[k])

        @pl.when(at_end)
        def _():
            take(coarse_all.at[k, 1], far_sem.at[k])

        def in_order(blocks_of):
            parts = [blocks_of[i * chips:(i + 1) * chips] for i in range(CORES)]
            return jnp.stack(parts, axis=1).reshape(n_sub * nc, goals)

        own = in_order(coarse_all[k, 0])
        beside = in_order(coarse_all[k, jnp.where(at_end, 1, 0)])
        dot = functools.partial(jnp.dot, precision=lax.Precision.HIGHEST, preferred_element_type=F32)
        return dot(inv[0], own), dot(inv[1], beside)

    loads[0].wait()
    loads[1].wait()
    loads[2].wait()
    loads[3].wait()
    own_par[pl.ds(nc, 8)] = jnp.concatenate([weight_v[...], occ_v[...].astype(F32), jnp.zeros((6, face), F32)], axis=0)

    def split_rows(rows):
        high, low = split(rows)
        return jnp.concatenate([high, low], axis=0)

    own_basis = split_rows(own_par[0:nc])
    coarse = jnp.zeros((2 * nc, 2 * goals), F32)
    for row in range(0, face, CH):
        high, low = split(res[pl.ds(row, CH)])
        half_b[pl.ds(row, CH)] = high
        coarse += jnp.dot(own_basis[:, row:row + CH], jnp.concatenate([high, low], axis=1), preferred_element_type=F32)

    def unsplit(value, rows):
        both = value[:, :goals] + value[:, goals:]
        return both[:rows] + both[rows:]

    first_coarse = unsplit(coarse, nc)

    line = lax.broadcasted_iota(jnp.int32, (8 * nc, 2 * goals), 0)
    lane = lax.broadcasted_iota(jnp.int32, (8 * nc, 2 * goals), 1)
    is_weight = jnp.logical_and(line >= 6 * nc, jnp.logical_and(line < 6 * nc + 3, lane < goals))
    is_free = jnp.logical_and(line == 6 * nc + 3, lane >= goals)
    pick = jnp.logical_or(is_weight, is_free).astype(F32).astype(BF16)

    def prepare(base, params):
        basis, wrow, frow = params[0:nc], params[nc:nc + 1], params[nc + 1:nc + 2]
        high, low = split(basis)
        fhigh, flow = split(basis * frow)
        whigh = wrow.astype(BF16).astype(F32)
        wmid = (wrow - whigh).astype(BF16).astype(F32)
        rest = [whigh, wmid, wrow - whigh - wmid, frow]
        tall = [high, high, low, low, fhigh, flow]
        tall = jnp.concatenate([t.astype(F32) for t in tall] + rest + [jnp.zeros((2 * nc - 4, face), F32)], axis=0)
        for col in range(0, face, 128):
            span = pl.ds(base + col, 128)
            cols = jnp.transpose(tall[:, col:col + 128]).astype(BF16)
            basis_t[span] = cols
            both = jnp.dot(cols, pick, preferred_element_type=F32)
            weight[span] = both[:, :goals]
            free[span] = both[:, goals:]
            some, none = cols[:, 4 * nc:6 * nc], jnp.zeros((128, 2 * nc), BF16)
            basis_f[span] = jnp.concatenate([some, none] if base == 0 else [none, some], axis=1)

    params = own_par[...]
    prepare(0, params)
    basis_n[...] = split_rows(params[0:nc] * (1.0 - params[nc + 1:nc + 2]))

    def weighted(i, span):
        high, low = split(free[span] * (weight[span] * res[span]))
        here = place(i * CH)
        alone[here, 0:goals] = high
        alone[here, goals:2 * goals] = low

    def weighted_own(i, carry):
        weighted(i, place(i * CH))
        return carry

    lax.fori_loop(0, face // CH, weighted_own, 0)
    loads[5].wait()

    def half_own(i, carry):
        span = place(i * CH)
        left = blocks[span, 0:face]
        y = jnp.dot(left, alone[...], preferred_element_type=F32)
        prod[span] = y[:, :goals] + y[:, goals:]
        qsum[span] = jnp.dot(left, basis_f[0:face], preferred_element_type=F32)
        return carry

    lax.fori_loop(0, 2 * face // CH, half_own, 0)
    pl.semaphore_wait(barrier, 2 + (chips - 1) + (n_near - 1) + (n_far - 1) + jnp.where(at_end, n_sub + 1, 1))
    remote(own_par, next_par, send_sem.at[2, 0], par_sem, prev_s, prev_g).start()
    gather_coarse(0, first_coarse)
    remote(half_b, held, send_sem.at[4, 0], half_sem, prev_s, prev_g).start()
    loads[4].wait()
    remote(inv.at[0], inv.at[1], send_sem.at[3, 0], inv_sem, prev_s, prev_g).start()
    take(next_par, par_sem)
    prepare(face, next_par[...] * has_next)

    def through(i, carry):
        span = place(i * CH)
        out = qsum[span] + jnp.dot(blocks[span, face:2 * face], basis_f[face:2 * face], preferred_element_type=F32)
        out = jnp.transpose(out)
        high, low = split(jnp.concatenate([out[0:nc] + out[nc:2 * nc], out[2 * nc:3 * nc] + out[3 * nc:]], axis=0))
        qmat[:, span] = jnp.concatenate([high, low], axis=0)
        high, low = high.astype(F32), low.astype(F32)
        qcol[span] = jnp.transpose(jnp.concatenate([high, high, low, low], axis=0)).astype(BF16)
        return carry

    lax.fori_loop(0, 2 * face // CH, through, 0)
    swap_coarse(0)
    take(inv.at[1], inv_sem)

    def stage_spread(which, value):
        high, low = split(value)
        spread_rhs[which] = jnp.concatenate([high, low, high, low, jnp.zeros((4 * nc, goals), BF16)], axis=0)

    def build(span, which, r):
        z = weight[span] * r + jnp.dot(basis_t[span], spread_rhs[which], preferred_element_type=F32)
        fz = free[span] * z
        high, low = split(fz)
        masked[span, 0:goals] = high
        masked[span, goals:2 * goals] = low
        zed[span] = z
        return z, fz

    zero8 = jnp.zeros((8, goals), F32)
    solved, solved_next = solve_coarse(0)
    stage_spread(0, solved)
    stage_spread(1, solved_next)
    high, low = split(jnp.concatenate([solved, solved_next], axis=0))
    solved_rhs[...] = jnp.concatenate([high, low, high, low], axis=0)

    def leftover(span, rest):
        high, low = split(rest)
        prob[span, 0:goals] = high
        prob[span, goals:2 * goals] = low

    def first_own(i, carry):
        gamma, delta = carry
        span = place(i * CH)
        r = res[span]
        z, fz = build(span, 0, r)
        rest = z - fz
        leftover(span, rest)
        return gamma + folded(r * z), delta + folded(rest * z)

    gamma, delta = lax.fori_loop(0, face // CH, first_own, (zero8, zero8))
    eps = zero8
    take(held, half_sem)

    def first_next(i, carry):
        span = place(face + i * CH)
        r = held[place(i * CH)].astype(F32) * has_next
        res[span] = r
        build(span, 1, r)
        weighted(i, span)
        return carry

    lax.fori_loop(0, face // CH, first_next, 0)

    gamma_old = p_ap = None
    for k in range(ITERS):
        more = k + 1 < ITERS
        if more:
            out = jnp.dot(qmat[...], masked[...], preferred_element_type=F32)
            part = jnp.dot(basis_n[...], prob[...], preferred_element_type=F32)
            out = out[:, :goals] + out[:, goals:]
            out = out[:2 * nc] + out[2 * nc:]
            kap_src[k] = out[nc:]
            remote(kap_src.at[k], kap_in.at[k], send_sem.at[5, k], kap_sem.at[k], next_s, next_g).start()
            part = unsplit(part, nc) + out[:nc]

        def rows_of(row, acc):
            span = place(row, TALL)
            if k == 0:
                y = jnp.dot(blocks[span, face:2 * face], alone[...], preferred_element_type=F32)
                y = prod[span] + y[:, :goals] + y[:, goals:]
                y += jnp.dot(qcol[span], solved_rhs[...], preferred_element_type=F32)
            else:
                y = jnp.dot(blocks[span], masked[...], preferred_element_type=F32)
                y = y[:, :goals] + y[:, goals:]
            prod[span] = y
            leave[k, span] = y.astype(BF16)
            return acc + folded(free[span] * zed[span] * y)

        def pair(i, acc):
            acc = rows_of(face + i * TALL, acc)
            remote(
                leave.at[k, place(face + i * TALL, TALL)], arrive.at[k, place(i * TALL, TALL)],
                send_sem.at[6, k], bulk_sem.at[k, 0], next_s, next_g,
            ).start()
            acc = rows_of(i * TALL, acc)
            if more:
                remote(
                    leave.at[k, place(i * TALL, TALL)], arrive.at[k, place(face + i * TALL, TALL)],
                    send_sem.at[7, k], bulk_sem.at[k, 1], prev_s, prev_g,
                ).start()
            return acc

        delta = lax.fori_loop(0, face // TALL, pair, delta)
        dots = [jnp.sum(v, axis=0, keepdims=True) for v in (gamma, delta, eps)]
        dots = jnp.concatenate(dots + [jnp.zeros((1, goals), F32)], axis=0)
        dot_src[k] = dots
        dot_grp[k, pl.ds(my_near, 1)] = dots[None]

        def to_grp(j, carry):
            remote(dot_src.at[k], dot_grp.at[k, my_near], send_sem.at[8, k], grp_sem.at[k], *near(j)).start()
            return carry

        lax.fori_loop(1, n_near, to_grp, 0)
        if more:
            take(kap_in.at[k], kap_sem.at[k])
            gather_coarse(k + 1, part + kap_in[k] * has_prev)
        take(dot_grp.at[k, pl.ds(0, n_near - 1)], grp_sem.at[k])
        dots = jnp.sum(dot_grp[k], axis=0)
        dot_mid[k] = dots
        dot_sub[k, pl.ds(my_far, 1)] = dots[None]

        def to_sub(j, carry):
            remote(dot_mid.at[k], dot_sub.at[k, my_far], send_sem.at[9, k], sub_sem.at[k], *far(j)).start()
            return carry

        lax.fori_loop(1, n_far, to_sub, 0)
        if more:
            swap_coarse(k + 1)
            moved, moved_next = solve_coarse(k + 1)
            stage_spread(0, moved)
            stage_spread(1, moved_next)
        take(arrive.at[k, pl.ds(0, face)], bulk_sem.at[k, 0])
        if more:
            take(arrive.at[k, pl.ds(face, face)], bulk_sem.at[k, 1])

        def apply(span, came, which):
            fr = free[span]
            w = fr * (prod[span] + came) + (1.0 - fr) * zed[span]
            if more:
                vee[span] = weight[span] * w + jnp.dot(basis_t[span], spread_rhs[which], preferred_element_type=F32)
            return w

        def apply_own(i, carry):
            span = place(i * CH)
            prod[span] = apply(span, arrive[k, span].astype(F32) * has_prev, 0)
            return carry

        def apply_next(i, carry):
            span = place(face + i * CH)
            apply(span, arrive[k, span].astype(F32), 1)
            return carry

        lax.fori_loop(0, face // CH, apply_own, 0)
        if more:
            lax.fori_loop(0, face // CH, apply_next, 0)
        take(dot_sub.at[k, pl.ds(0, n_far - 1)], sub_sem.at[k])
        dots = jnp.sum(dot_sub[k], axis=0)
        gamma_now, delta_now, eps_now = dots[0:1], dots[1:2], dots[2:3]
        if k == 0:
            p_ap = delta_now
            beta = None
        else:
            beta = gamma_now / gamma_old
            p_ap = delta_now + beta * (2.0 * eps_now + beta * p_ap)
        alpha = gamma_now / p_ap
        gamma_old = gamma_now

        def turn(span):
            t = vee[span] if k == 0 else vee[span] + beta * tee[span]
            if k + 2 < ITERS:
                tee[span] = t
            z = zed[span] - alpha * t
            zed[span] = z
            fz = free[span] * z
            high, low = split(fz)
            masked[span, 0:goals] = high
            masked[span, goals:2 * goals] = low
            return z, z - fz

        def own_rows(i, carry):
            gamma, delta, eps = carry
            span = place(i * CH)
            sr = prod[span] if k == 0 else prod[span] + beta * srch[span]
            r = res[span] - alpha * sr
            d = zed[span] if k == 0 else zed[span] + beta * direc[span]
            x = alpha * d if k == 0 else x_ref[span] + alpha * d
            x_ref[span] = x
            if not more:
                r_ref[span] = r
                pltpu.make_async_copy(x_ref.at[span], x_out.at[span], out_sem.at[0, i]).start()
                pltpu.make_async_copy(r_ref.at[span], r_out.at[span], out_sem.at[1, i]).start()
                return carry
            direc[span] = d
            srch[span] = sr
            res[span] = r
            z, rest = turn(span)
            if k + 2 < ITERS:
                leftover(span, rest)
            return gamma + folded(r * z), delta + folded(rest * z), eps + folded(z * sr)

        gamma, delta, eps = lax.fori_loop(0, face // CH, own_rows, (zero8, zero8, zero8))
        if more:
            def next_rows(i, carry):
                turn(place(face + i * CH))
                return carry

            lax.fori_loop(0, face // CH, next_rows, 0)

    for i in range(face // CH):
        pltpu.make_async_copy(x_ref.at[pl.ds(i * CH, CH)], x_out.at[pl.ds(i * CH, CH)], out_sem.at[0, i]).wait()
        pltpu.make_async_copy(r_ref.at[pl.ds(i * CH, CH)], r_out.at[pl.ds(i * CH, CH)], out_sem.at[1, i]).wait()
    for k in range(ITERS):
        take(coarse_all.at[k, 0, pl.ds(0, chips - 1)], send_sem.at[0, k])
        take(coarse_all.at[k, 0, mine], send_sem.at[10, k])
        take(coarse_src.at[k], send_sem.at[1, k])
        take(leave.at[k, pl.ds(face, face)], send_sem.at[6, k])
        if k + 1 < ITERS:
            take(leave.at[k, pl.ds(0, face)], send_sem.at[7, k])
            take(kap_src.at[k], send_sem.at[5, k])
        take(dot_grp.at[k, pl.ds(0, n_near - 1)], send_sem.at[8, k])
        take(dot_sub.at[k, pl.ds(0, n_far - 1)], send_sem.at[9, k])
    take(own_par, send_sem.at[2, 0])
    take(inv.at[0], send_sem.at[3, 0])
    take(half_b, send_sem.at[4, 0])


def ship(x_in, r_in, x_out, r_out, held, sem):
    moves = []
    for which, (src, dst) in enumerate(((x_in, x_out), (r_in, r_out))):
        for i in range(src.shape[0] // CH):
            span = pl.ds(i * CH, CH)
            inward = pltpu.make_async_copy(src.at[span], held.at[which, span], sem.at[0, which, i])
            outward = pltpu.make_async_copy(held.at[which, span], dst.at[span], sem.at[1, which, i])
            inward.start()
            moves.append((inward, outward))
    for inward, outward in moves:
        inward.wait()
        outward.start()
    for inward, outward in moves:
        outward.wait()


def solution(mesh):
    n_sub, n_grp = mesh.shape["sub"], mesh.shape["grp"]

    def local(right_side, schur_blocks, occupancy, precond_weights, coarse_basis, coarse_inverse):
        face, goals = right_side.shape[2:]
        nc = coarse_basis.shape[2]
        both = 2 * face
        dma = pltpu.SemaphoreType.DMA
        out = jax.ShapeDtypeStruct((face, goals), F32)
        x, r = pl.pallas_call(
            functools.partial(kernel, n_sub, n_grp),
            out_shape=(out, out),
            in_specs=[pl.BlockSpec(memory_space=pl.ANY)] * 6,
            out_specs=[pl.BlockSpec(memory_space=pl.ANY)] * 2,
            scratch_shapes=[
                pltpu.VMEM((face, goals), F32),
                pltpu.VMEM((face, goals), F32),
                pltpu.VMEM((both, both), BF16),
                pltpu.VMEM((both, goals), F32),
                pltpu.VMEM((both, goals), F32),
                pltpu.VMEM((both, goals), F32),
                pltpu.VMEM((both, goals), F32),
                pltpu.VMEM((both, goals), F32),
                pltpu.VMEM((both, goals), F32),
                pltpu.VMEM((both, goals), F32),
                pltpu.VMEM((both, goals), F32),
                pltpu.VMEM((both, 2 * goals), BF16),
                pltpu.VMEM((face, goals), BF16),
                pltpu.VMEM((ITERS, both, goals), BF16),
                pltpu.VMEM((ITERS, both, goals), BF16),
                pltpu.VMEM((face, goals), BF16),
                pltpu.VMEM((nc + 8, face), F32),
                pltpu.VMEM((nc + 8, face), F32),
                pltpu.VMEM((1, face), jnp.int32),
                pltpu.VMEM((1, face), F32),
                pltpu.VMEM((2, nc, n_sub * nc), F32),
                pltpu.VMEM((both, 8 * nc), BF16),
                pltpu.VMEM((2, 8 * nc, goals), BF16),
                pltpu.VMEM((face, 2 * goals), BF16),
                pltpu.VMEM((4 * nc, both), BF16),
                pltpu.VMEM((2 * nc, face), BF16),
                pltpu.VMEM((both, 4 * nc), BF16),
                pltpu.VMEM((face, 2 * goals), BF16),
                pltpu.VMEM((both, 4 * nc), F32),
                pltpu.VMEM((both, 8 * nc), BF16),
                pltpu.VMEM((8 * nc, goals), BF16),
                pltpu.VMEM((face, goals), F32),
                pltpu.VMEM((ITERS, nc, goals), F32),
                pltpu.VMEM((ITERS, 2, n_sub, nc, goals), F32),
                pltpu.VMEM((ITERS, nc, goals), F32),
                pltpu.VMEM((ITERS, nc, goals), F32),
                pltpu.VMEM((ITERS, 4, goals), F32),
                pltpu.VMEM((ITERS, PLANE * ROW, 4, goals), F32),
                pltpu.VMEM((ITERS, 4, goals), F32),
                pltpu.VMEM((ITERS, n_sub * n_grp // (PLANE * ROW), 4, goals), F32),
                dma((6,)),
                dma((11, ITERS)),
                dma,
                dma,
                dma,
                dma((ITERS, 2)),
                dma((ITERS,)),
                dma((ITERS,)),
                dma((ITERS,)),
                dma((ITERS,)),
                dma((ITERS,)),
                dma((2, face // CH)),
                dma((ITERS,)),
            ],
            compiler_params=pltpu.CompilerParams(
                collective_id=0, has_side_effects=True, vmem_limit_bytes=60 << 20
            ),
        )(right_side[0, 0], schur_blocks[0, 0], occupancy[0], precond_weights[0], coarse_basis[0, 0], coarse_inverse[0])
        x, r = pl.pallas_call(
            ship,
            out_shape=(out, out),
            in_specs=[pl.BlockSpec(memory_space=pl.ANY)] * 2,
            out_specs=[pl.BlockSpec(memory_space=pl.ANY)] * 2,
            scratch_shapes=[pltpu.VMEM((2, face, goals), F32), dma((2, 2, face // CH))],
        )(x, r)
        return x[None, None], r[None, None]

    return jax.shard_map(
        local,
        mesh=mesh,
        in_specs=(
            P("grp", "sub", None, None),
            P("grp", "sub", None, None),
            P("grp", "sub", None),
            P("grp", "sub", None),
            P("grp", "sub", None, None),
            P("grp", "sub", None),
        ),
        out_specs=(P("grp", "sub", None, None), P("grp", "sub", None, None)),
        check_vma=False,
    )
```
